32 devices in a mesh: groups: 1, dp: 32 (over z, y, x, core).
Axes of the slice: x: 2, y: 2, z: 4, core: 2. Of those that a mesh axis runs over, the one named last changes fastest.
Arguments:
- activations: bfloat16 [128, 8192], P(('groups', 'dp')), may hold values from -6 to 6
- cotangent: bfloat16 [128, 8192], P(('groups', 'dp')), may hold values from -6 to 6
- w_gate: bfloat16 [28672, 8192], P('dp'), may hold values from -0.0625 to 0.0625
- w_up: bfloat16 [28672, 8192], P('dp'), may hold values from -0.0625 to 0.0625
- w_down: bfloat16 [28672, 8192], P('dp'), may hold values from -0.03125 to 0.03125
- proj_model: bfloat16 [8192, 192], P('dp'), may hold values from -0.0625 to 0.0625
- proj_hidden: bfloat16 [28672, 192], P('dp'), may hold values from -0.03125 to 0.03125
- seq_ids: int32 [128], P('groups'), may hold values from 0 to 15, never falling along the last dimension, each value on 1 to 16 neighbouring positions
- targets: bfloat16 [256, 3, 64, 64], P(('groups', 'dp')), may hold values from -24 to 24
- target_domain: int32 [256], P(('groups', 'dp')), may hold values from 0 to 31, never falling along the last dimension, each value on 1 to 16 neighbouring positions
Outputs:
- sketches: float32 [16, 3, 64, 64], P('groups')
- scores: float32 [16, 32], P('groups')
The draws below stay inside these ranges and needn't reach their ends.
Inputs may be any that keep to these rules, and one draw needn't show every extreme that they name: `seq_ids`: never falling along the tokens; each of the 16 sequences has 1 to 16 tokens, one exactly 16. `target_domain`: never falling along the target examples; each of the 32 domains has 1 to 16 examples, one exactly 16.
All inputs are finite; a program needn't handle non-finite values.
Results may differ from the reference program's by a relative error of at most 0.0032.
Values may be sent and summed in bfloat16 or wider, within the bound.
A program may use at most 128 MiB of HBM per device.

```python
import math
import jax
import jax.numpy as jnp
import numpy as np
from jax import lax

D = 8192
FF = 28672
RANK = 64
DOMAINS = 32
SEQS = 16
TOKENS = 128
TARGETS = 256
SEQ_MOST = 16
DOM_MOST = 16


def level_of(own_key, extent, cuts, low, top_value):
    loudness, own = 1.0, jax.random.fold_in(own_key, 6)
    for dim, blocks in cuts:
        steps = jnp.exp(jax.random.uniform(jax.random.fold_in(own, dim), (blocks,), jnp.float32, low / len(cuts), top_value / len(cuts)))
        loudness = loudness * jnp.repeat(steps, extent[dim] // blocks).reshape([-1 if axis == dim else 1 for axis in range(len(extent))])
    return loudness


def length_profile(amount, total, reach, skew):
    portions = [(1 << 20) // math.isqrt(rank ** skew) + 1 for rank in range(2, amount + 1)]
    rest, counts = total - reach - (amount - 1), [1] * (amount - 1)
    while rest > 0:
        candidates = [i for i in range(amount - 1) if counts[i] < reach]
        mass, budget = sum([portions[i] for i in candidates]), rest
        for i in candidates:
            extra = min(reach - counts[i], max(1, budget * portions[i] // mass), rest)
            counts[i] = counts[i] + extra
            rest = rest - extra
    return np.array([reach] + counts)


def ragged_sizes(rng, amount, total, limit, slope):
    if amount == 2:
        one = jax.random.randint(rng, (), max(1, total - limit), min(limit, total - 1) + 1)
        return jnp.stack([one, total - one])
    tallies = jnp.asarray(length_profile(amount, total, limit, slope), jnp.int32)
    couples = (amount - 1) // 2
    source_of, taker = tallies[1:1 + 2 * couples:2], tallies[2:2 + 2 * couples:2]
    room = jnp.minimum(source_of - 1, limit - taker)
    moved = jax.random.randint(jax.random.fold_in(rng, 1), (couples,), 0, 1 << 20) % (room + 1)
    tallies = tallies.at[1:1 + 2 * couples:2].set(source_of - moved).at[2:2 + 2 * couples:2].set(taker + moved)
    return tallies[jax.random.permutation(jax.random.fold_in(rng, 2), amount)]


def bell_draw(key, extent, spread, bound, shards=(), dtype=jnp.bfloat16):
    values = spread * jax.random.normal(key, extent, jnp.float32)
    if shards:
        values = values * level_of(key, extent, shards, -0.22, 0.18)
    return jnp.clip(values, -bound, bound).astype(dtype)


def setup_inputs(seed: int = 0, part: int = 0) -> dict:
    streams_of = jax.random.split(jax.random.key(seed), 11)
    part_splits = jax.random.split(jax.random.fold_in(streams_of[10], part), 11)
    activations = bell_draw(part_splits[0], (TOKENS, D), 1.0, 6.0, ((0, 32),))
    cotangent = bell_draw(part_splits[1], (TOKENS, D), 1.0, 6.0, ((0, 32),))
    w_gate = bell_draw(streams_of[2], (FF, D), D ** -0.5, 0.0625, ((0, 32),))
    w_up = bell_draw(streams_of[3], (FF, D), D ** -0.5, 0.0625, ((0, 32),))
    w_down = bell_draw(streams_of[4], (FF, D), FF ** -0.5, 0.03125, ((0, 32),))
    proj_model = bell_draw(streams_of[5], (D, 3 * RANK), D ** -0.5, 0.0625, ((0, 32),))
    proj_hidden = bell_draw(streams_of[6], (FF, 3 * RANK), FF ** -0.5, 0.03125, ((0, 32),))
    seq_ids = jnp.searchsorted(jnp.cumsum(ragged_sizes(part_splits[7], SEQS, TOKENS, SEQ_MOST, 2)), jnp.arange(TOKENS), side="right").astype(jnp.int32)
    targets = bell_draw(part_splits[8], (TARGETS, 3, RANK, RANK), 4.0, 24.0, ((0, 32),))
    target_domain = jnp.searchsorted(jnp.cumsum(ragged_sizes(part_splits[9], DOMAINS, TARGETS, DOM_MOST, 2)), jnp.arange(TARGETS), side="right").astype(jnp.int32)
    return dict(activations=activations, cotangent=cotangent, w_gate=w_gate, w_up=w_up, w_down=w_down, proj_model=proj_model, proj_hidden=proj_hidden, seq_ids=seq_ids, targets=targets, target_domain=target_domain)


def sequence_sketch(vectors, onehot):
    blocks = vectors.reshape(vectors.shape[0], 6, RANK)
    left_side = jnp.stack((blocks[:, 4], blocks[:, 5], blocks[:, 3]), 1)
    right_side = jnp.stack((blocks[:, 0], blocks[:, 1], blocks[:, 2]), 1)
    return jnp.einsum('ns,nka,nkb->skab', onehot, left_side, right_side, precision=lax.Precision.HIGHEST)

def reference(activations, cotangent, w_gate, w_up, w_down, proj_model, proj_hidden, seq_ids, targets, target_domain):
    pieces = 8
    width_block = FF // pieces
    in_model = jnp.dot(activations, proj_model[:, :2 * RANK], preferred_element_type=jnp.float32)
    out_down = jnp.dot(cotangent, proj_model[:, 2 * RANK:], preferred_element_type=jnp.float32)

    def hidden_block(inputs_block):
        gate_rows, up_rows, down_rows, proj_rows = inputs_block
        gate_value = jnp.dot(activations, gate_rows.T, preferred_element_type=jnp.float32)
        up_value = jnp.dot(activations, up_rows.T, preferred_element_type=jnp.float32)
        sigmoid_gate = jax.nn.sigmoid(gate_value)
        silu_gate = gate_value * sigmoid_gate
        hidden = (silu_gate * up_value).astype(jnp.bfloat16)
        grad_hidden = jnp.dot(cotangent, down_rows.T, preferred_element_type=jnp.float32)
        grad_gate = (grad_hidden * up_value * sigmoid_gate * (1.0 + gate_value * (1.0 - sigmoid_gate))).astype(jnp.bfloat16)
        grad_up = (grad_hidden * silu_gate).astype(jnp.bfloat16)
        in_down = jnp.dot(hidden, proj_rows[:, :RANK], preferred_element_type=jnp.float32)
        out_gate = jnp.dot(grad_gate, proj_rows[:, RANK:2 * RANK], preferred_element_type=jnp.float32)
        out_up = jnp.dot(grad_up, proj_rows[:, 2 * RANK:], preferred_element_type=jnp.float32)
        return jnp.concatenate([in_down, out_gate, out_up], 1)
    stacked = (w_gate.reshape(pieces, width_block, D), w_up.reshape(pieces, width_block, D), w_down.reshape(pieces, width_block, D), proj_hidden.reshape(pieces, width_block, 3 * RANK))
    hidden_terms = lax.optimization_barrier(jnp.sum(lax.map(hidden_block, stacked), axis=0))
    vectors = jnp.concatenate([in_model, out_down, hidden_terms], 1)
    onehot = (seq_ids[:, None] == jnp.arange(SEQS)[None, :]).astype(jnp.float32)
    sketches = sequence_sketch(vectors, onehot)
    flat_sketch = sketches.reshape(SEQS, 3 * RANK * RANK)
    domain_onehot = (target_domain[None, :] == jnp.arange(DOMAINS)[:, None]).astype(jnp.bfloat16)
    domain_sum = jnp.dot(domain_onehot, targets.reshape(TARGETS, 3 * RANK * RANK), preferred_element_type=jnp.float32)
    domain_count = lax.optimization_barrier(jnp.sum(domain_onehot.astype(jnp.float32), 1))
    domain_mean = domain_sum / domain_count[:, None]
    inverse_norm = lax.rsqrt(lax.optimization_barrier(jnp.sum(flat_sketch * flat_sketch, 1)) + 1e-06)
    scores = jnp.dot(flat_sketch, domain_mean.T, precision=lax.Precision.HIGHEST) * inverse_norm[:, None]
    return (sketches, scores)
```

```python
import functools

import jax
import jax.numpy as jnp
from jax import lax
from jax.experimental import pallas as pl
from jax.experimental.pallas import tpu as pltpu
from jax.sharding import PartitionSpec as P

DOMAINS = 32
SEQS = 16
MESH = pl.DeviceIdType.MESH
ROUTES = 2
CHUNKS = 8
TILE = 8


def routes_of(n):
    core = (2, 1)
    if n == 32:
        z, y, x = (4, 8), (2, 4), (2, 2)
        return ((z, y, x, core), (z, x, y, core))
    if n == 128:
        y, x = (8, 16), (8, 2)
        return ((y, x, core), (x, y, core))
    rest = (n // 2, 2)
    return ((rest, core), (rest, core))


def moved(index, size, stride, by):
    coord = lax.rem(lax.div(index, stride), size)
    return index + (lax.rem(coord + by, size) - coord) * stride


def kernel(
    n,
    act_ref, cot_ref, wg_ref, wu_ref, wd_ref, pm_ref, ph_ref, seq_ref, tgt_ref, dom_ref,
    sk_ref, score_ref,
    wbuf, xg, xs, gacc, uacc, dacc, pm, ph, tgt, tt, partl, partr, rsl, rsr, redl, redr, vl, vr, lm, msg, msgbuf,
    w_sem, own_sem, in_sem, ag_send, ag_recv, rs_send, rs_recv, bc_send, bc_recv, sc_send, sc_recv,
):
    me = lax.axis_index("dp")
    routes = routes_of(n)
    stages = len(routes[0])
    tokens, width = xs.shape[2], xs.shape[3]
    half_width = width // ROUTES
    rank = pm_ref.shape[0] // 3
    hidden_units = wg_ref.shape[0]
    own_rows = act_ref.shape[2]
    examples = tgt_ref.shape[0]
    tiles = partl.shape[0]

    def mult(r, stage):
        count = 1
        for size, _ in routes[r][:stage]:
            count = count * size
        return count

    def position(r, index, first=0):
        total = 0
        for i, (size, stride) in enumerate(routes[r]):
            if i >= first:
                if isinstance(index, int):
                    total += index // stride % size * mult(r, i)
                else:
                    total += lax.rem(lax.div(index, stride), size) * mult(r, i)
        return total

    def weight_copy(m, c):
        source = (wg_ref, wu_ref, wd_ref)[m]
        return pltpu.make_async_copy(
            source.at[:, pl.ds(c * width, width)], wbuf.at[m, c], w_sem.at[m, c]
        )

    own_copies = []
    for a, source in enumerate((act_ref, cot_ref)):
        for r in range(ROUTES):
            copy = pltpu.make_async_copy(
                source.at[:, r], xg.at[:, r, position(r, me), a], own_sem.at[a, r]
            )
            copy.start()
            own_copies.append(copy)

    barrier = pltpu.get_barrier_semaphore()
    partners = 0
    for size, stride in routes[0]:
        for d in range(1, size):
            pl.semaphore_signal(
                barrier, inc=1, device_id={"dp": moved(me, size, stride, d)}, device_id_type=MESH
            )
            partners += 1
    in_copies = [
        pltpu.make_async_copy(source, target, in_sem.at[i])
        for i, (source, target) in enumerate(((pm_ref, pm), (ph_ref, ph), (tgt_ref, tgt)))
    ]
    for m in range(3):
        weight_copy(m, 0).start()
    for copy in own_copies:
        copy.wait()
    pl.semaphore_wait(barrier, partners)

    def send_stage(c, r, stage):
        size, stride = routes[r][stage]
        blocks = xg.at[c, r, pl.ds(position(r, me, stage), mult(r, stage))]
        for d in range(1, size):
            pltpu.make_async_remote_copy(
                src_ref=blocks,
                dst_ref=blocks,
                send_sem=ag_send.at[r],
                recv_sem=ag_recv.at[c, r, stage],
                device_id={"dp": moved(me, size, stride, d)},
                device_id_type=MESH,
            ).start()

    def take_stage(c, r, stage):
        blocks = xg.at[c, r, pl.ds(0, mult(r, stage) * (routes[r][stage][0] - 1))]
        pltpu.make_async_copy(blocks, blocks, ag_recv.at[c, r, stage]).wait()

    def relay(c, stage):
        for r in range(ROUTES):
            take_stage(c, r, stage - 1)
            send_stage(c, r, stage)

    def first_sends(c, carry):
        for r in range(ROUTES):
            send_stage(c, r, 0)
        return carry

    def later_weights(c, carry):
        for m in range(3):
            weight_copy(m, c).start()
        return carry

    lax.fori_loop(0, CHUNKS, first_sends, 0)
    lax.fori_loop(1, CHUNKS, later_weights, 0)
    for copy in in_copies:
        copy.start()
    gacc[...] = jnp.zeros_like(gacc)
    uacc[...] = jnp.zeros_like(uacc)
    dacc[...] = jnp.zeros_like(dacc)

    def lay_out(a, c):
        group = 16 // own_rows
        for r in range(ROUTES):
            for g in range(tokens // 16):
                pieces = [
                    xg[c, r, position(r, g * group + i), a].astype(jnp.float32) for i in range(group)
                ]
                xs[a, c, g * 16 : (g + 1) * 16, r * half_width : (r + 1) * half_width] = jnp.concatenate(
                    pieces, 0
                ).astype(jnp.bfloat16)

    contract = (((1,), (1,)), ((), ()))

    def add_product(acc, a, m, c):
        weight_copy(m, c).wait()
        acc[...] += lax.dot_general(
            wbuf[m, c], xs[a, c], contract, preferred_element_type=jnp.float32
        )

    for lead in range(1, stages):
        for stage in range(1, lead + 1):
            relay(lead - stage, stage)

    def step(c, last=CHUNKS):
        relays = [(c + stages - stage, stage) for stage in range(stages - 1, 0, -1)]
        relays = [pair for i, pair in enumerate(relays) if i + 1 < last]
        for pair in relays[:1]:
            relay(*pair)
        for r in range(ROUTES):
            take_stage(c, r, stages - 1)
        lay_out(0, c)
        add_product(gacc, 0, 0, c)
        for pair in relays[1:2]:
            relay(*pair)
        add_product(uacc, 0, 1, c)
        for pair in relays[2:]:
            relay(*pair)
        lay_out(1, c)
        add_product(dacc, 1, 2, c)

    def looped(c, carry):
        step(c)
        return carry

    steady = CHUNKS - stages + 1
    lax.fori_loop(0, steady, looped, 0)
    for c in range(steady, CHUNKS):
        step(c, CHUNKS - c)

    for copy in in_copies:
        copy.wait()
    window = pm_ref.shape[1]
    model_cols = CHUNKS * width // n
    start = lax.div(me * model_cols, window) * window
    own_chunk = lax.div(start, width)
    own_cols = pl.ds(pl.multiple_of(lax.rem(start, width), window), window)

    def tiled(x):
        return x.reshape(x.shape[0] // TILE, TILE, tokens)

    split = 2 * rank // TILE
    partr[:split] = tiled(
        lax.dot_general(
            pm[: 2 * rank, :], xs[0, own_chunk, :, own_cols], contract, preferred_element_type=jnp.float32
        )
    )
    partr[split:] = tiled(
        lax.dot_general(
            pm[2 * rank :, :], xs[1, own_chunk, :, own_cols], contract, preferred_element_type=jnp.float32
        )
    )

    def owner_of(side, tile):
        owner = lax.div(tile * n, tiles)
        return n - 1 - owner if side else owner

    def side_of(side):
        index = n - 1 - me if side else me
        part, rsbuf, red, v = ((partl, rsl, redl, vl), (partr, rsr, redr, vr))[side]
        near = lax.div(index * tiles, n)
        mine = lax.div(index * tiles + n - 1, n)
        reduces = lax.div(mine * n, tiles) == index
        return part, rsbuf, red, v, near, mine, reduces

    def scatter(side):
        part, rsbuf, _, _, near, _, _ = side_of(side)

        def one(d, carry):
            tile = lax.rem(near + d, tiles)
            owner = owner_of(side, tile)

            @pl.when(owner == me)
            def _():
                pltpu.make_async_copy(part.at[tile], rsbuf.at[me], rs_recv.at[side]).start()

            @pl.when(owner != me)
            def _():
                pltpu.make_async_remote_copy(
                    src_ref=part.at[tile],
                    dst_ref=rsbuf.at[me],
                    send_sem=rs_send.at[side],
                    recv_sem=rs_recv.at[side],
                    device_id={"dp": owner},
                    device_id_type=MESH,
                ).start()

            return carry

        lax.fori_loop(0, tiles, one, 0)

    def share(side):
        part, rsbuf, red, v, _, mine, reduces = side_of(side)

        @pl.when(reduces)
        def _():
            pltpu.make_async_copy(rsbuf, rsbuf, rs_recv.at[side]).wait()
            red[...] = jnp.sum(rsbuf[...], 0)
            pltpu.make_async_copy(red, v.at[mine], bc_recv.at[side]).start()

            def one(d, carry):
                pltpu.make_async_remote_copy(
                    src_ref=red,
                    dst_ref=v.at[mine],
                    send_sem=bc_send.at[side],
                    recv_sem=bc_recv.at[side],
                    device_id={"dp": lax.rem(me + d, n)},
                    device_id_type=MESH,
                ).start()
                return carry

            lax.fori_loop(1, n, one, 0)

    def settle(side):
        part, rsbuf, red, v, _, _, reduces = side_of(side)

        @pl.when(reduces)
        def _():
            sent = part.at[pl.ds(0, tiles - 1)]
            pltpu.make_async_copy(sent, sent, rs_send.at[side]).wait()
            sent = rsbuf.at[pl.ds(0, n - 1)]
            pltpu.make_async_copy(sent, sent, bc_send.at[side]).wait()

        @pl.when(jnp.logical_not(reduces))
        def _():
            pltpu.make_async_copy(part, part, rs_send.at[side]).wait()

    scatter(1)
    in_down = out_gate = out_up = jnp.zeros((rank, tokens), jnp.float32)
    for off in range(0, hidden_units, 256):
        rows = slice(off, min(off + 256, hidden_units))
        gate, up, grad = gacc[rows], uacc[rows], dacc[rows]
        sig = jax.nn.sigmoid(gate)
        silu = gate * sig
        hidden = (silu * up).astype(jnp.bfloat16)
        grad_gate = (grad * up * sig * (1.0 + gate * (1.0 - sig))).astype(jnp.bfloat16)
        grad_up = (grad * silu).astype(jnp.bfloat16)
        in_down += jnp.dot(ph[:rank, rows], hidden, preferred_element_type=jnp.float32)
        out_gate += jnp.dot(ph[rank : 2 * rank, rows], grad_gate, preferred_element_type=jnp.float32)
        out_up += jnp.dot(ph[2 * rank :, rows], grad_up, preferred_element_type=jnp.float32)
    third = rank // TILE
    partl[:third] = tiled(out_gate)
    partl[third : 2 * third] = tiled(out_up)
    partl[2 * third :] = tiled(in_down)
    scatter(0)

    for e in range(examples):
        for k in range(3):
            piece = tgt[e, k].astype(jnp.float32)
            tt[k, e * rank : (e + 1) * rank, :] = jnp.concatenate([piece, piece], 1).astype(jnp.bfloat16)
    share(1)
    share(0)
    seq = seq_ref[...]
    lanes = lax.broadcasted_iota(jnp.int32, (1, examples * SEQS), 1)
    domains = jnp.zeros((1, examples * SEQS), jnp.int32)
    for e in range(examples):
        domains = jnp.where(lax.div(lanes, SEQS) == e, dom_ref[e], domains)
    msg[1:2] = domains.astype(jnp.float32)
    same = lax.broadcasted_iota(jnp.int32, (examples * SEQS, tokens), 0)
    same = jnp.where(lax.rem(same, SEQS) == seq, 1.0, 0.0).astype(jnp.bfloat16)

    pltpu.make_async_copy(vr, vr, bc_recv.at[1]).wait()
    rights = []
    products = []
    for k in range(3):
        right = vr[k * third : (k + 1) * third].reshape(rank, tokens)
        hi = right.astype(jnp.bfloat16)
        lo = (right - hi.astype(jnp.float32)).astype(jnp.bfloat16)
        rights.append((hi, lo))
        products.append(
            jnp.dot(tt[k], jnp.concatenate([hi, lo], 0), preferred_element_type=jnp.float32)
        )
    pltpu.make_async_copy(vl, vl, bc_recv.at[0]).wait()
    lefts = [vl[k * third : (k + 1) * third].reshape(rank, tokens) for k in range(3)]
    terms = jnp.zeros((examples, rank, tokens), jnp.float32)
    for k in range(3):
        terms += products[k].reshape(examples, rank, tokens) * lefts[k][None]
    term = jnp.sum(terms, 1)
    term_hi = term.astype(jnp.bfloat16).astype(jnp.float32)
    term_mid = (term - term_hi).astype(jnp.bfloat16).astype(jnp.float32)
    term_lo = term - term_hi - term_mid
    summed = lax.dot_general(
        jnp.concatenate([term_hi, term_mid, term_lo], 0).astype(jnp.bfloat16), same, contract,
        preferred_element_type=jnp.float32,
    )
    summed = summed[:examples] + summed[examples : 2 * examples] + summed[2 * examples :]
    row = lax.broadcasted_iota(jnp.int32, summed.shape, 0)
    lane = lax.broadcasted_iota(jnp.int32, summed.shape, 1)
    msg[0:1] = jnp.sum(jnp.where(lax.div(lane, SEQS) == row, summed, 0.0), 0, keepdims=True)
    pltpu.make_async_copy(msg, msgbuf.at[me], sc_recv).start()

    def spread(d, carry):
        pltpu.make_async_remote_copy(
            src_ref=msg,
            dst_ref=msgbuf.at[me],
            send_sem=sc_send,
            recv_sem=sc_recv,
            device_id={"dp": lax.rem(me + d, n)},
            device_id_type=MESH,
        ).start()
        return carry

    lax.fori_loop(1, n, spread, 0)

    squares = jnp.zeros((SEQS, TILE, rank), jnp.float32)
    for k in range(3):
        left_hi = lefts[k].astype(jnp.bfloat16).astype(jnp.float32)
        left_lo = lefts[k] - left_hi
        for s in range(SEQS):
            here = seq == s
            hi = jnp.where(here, left_hi, 0.0).astype(jnp.bfloat16)
            lo = jnp.where(here, left_lo, 0.0).astype(jnp.bfloat16)
            block = slice(s * rank, (s + 1) * rank)
            lm[block, :tokens] = hi
            lm[block, tokens : 2 * tokens] = lo
            lm[block, 2 * tokens :] = hi
        hi, lo = rights[k]
        sketch = lax.dot_general(
            lm[...], jnp.concatenate([hi, hi, lo], 1), contract, preferred_element_type=jnp.float32
        ).reshape(SEQS, rank, rank)
        sk_ref[:, k] = sketch
        for i in range(0, rank, TILE):
            piece = sketch[:, i : i + TILE]
            squares = squares + piece * piece
    inverse_norm = lax.rsqrt(jnp.sum(jnp.sum(squares, 1), 1, keepdims=True) + 1e-06)

    for side in range(2):
        settle(side)

    def sent_chunk(c, carry):
        for r in range(ROUTES):
            sent = xg.at[c, r, pl.ds(0, n - 1)]
            pltpu.make_async_copy(sent, sent, ag_send.at[r]).wait()
        return carry

    lax.fori_loop(0, CHUNKS, sent_chunk, 0)
    sent = msgbuf.at[pl.ds(0, n - 1)]
    pltpu.make_async_copy(sent, sent, sc_send).wait()
    pltpu.make_async_copy(msgbuf, msgbuf, sc_recv).wait()
    domain = lax.broadcasted_iota(jnp.int32, (DOMAINS, examples * SEQS), 0).astype(jnp.float32)
    total = jnp.zeros(domain.shape, jnp.float32)
    counts = jnp.zeros(domain.shape, jnp.float32)
    for i in range(n):
        got = msgbuf[i]
        here = got[1:2] == domain
        total += jnp.where(here, got[0:1], 0.0)
        counts += jnp.where(here, 1.0, 0.0)
    shift = SEQS
    while shift < examples * SEQS:
        total += pltpu.roll(total, shift, 1)
        counts += pltpu.roll(counts, shift, 1)
        shift *= 2
    score_ref[...] = (total / counts).T[:SEQS] * inverse_norm


def on_device(n, activations, cotangent, w_gate, w_up, w_down, proj_model, proj_hidden, seq_ids, targets, target_domain):
    own_rows, model = activations.shape
    tokens = n * own_rows
    hidden_units = w_gate.shape[0]
    model_cols, features = proj_model.shape
    rank = features // 3
    width = model // CHUNKS
    stages = len(routes_of(n)[0])
    examples = targets.shape[0]
    tiles = features // TILE

    def by_chunk(x):
        return x.reshape(own_rows, CHUNKS, ROUTES, width // ROUTES).transpose(1, 2, 0, 3)

    proj_model, proj_hidden = proj_model.T, proj_hidden.T
    if model_cols < 128:
        me = lax.axis_index("dp")
        padded = jnp.zeros((features, 128), proj_model.dtype)
        proj_model = lax.dynamic_update_slice(padded, proj_model, (0, (me * model_cols) % 128))
    vmem = pl.BlockSpec(memory_space=pltpu.VMEM)
    hbm = pl.BlockSpec(memory_space=pl.ANY)
    smem = pl.BlockSpec(memory_space=pltpu.SMEM)
    f32, bf16 = jnp.float32, jnp.bfloat16
    dma = pltpu.SemaphoreType.DMA
    return pl.pallas_call(
        functools.partial(kernel, n),
        out_shape=(
            jax.ShapeDtypeStruct((SEQS, 3, rank, rank), f32),
            jax.ShapeDtypeStruct((SEQS, DOMAINS), f32),
        ),
        in_specs=[hbm, hbm, hbm, hbm, hbm, hbm, hbm, vmem, hbm, smem],
        out_specs=(vmem, vmem),
        scratch_shapes=[
            pltpu.VMEM((3, CHUNKS, hidden_units, width), bf16),
            pltpu.VMEM((CHUNKS, ROUTES, n, 2, own_rows, width // ROUTES), bf16),
            pltpu.VMEM((2, CHUNKS, tokens, width), bf16),
            pltpu.VMEM((hidden_units, tokens), f32),
            pltpu.VMEM((hidden_units, tokens), f32),
            pltpu.VMEM((hidden_units, tokens), f32),
            pltpu.VMEM(proj_model.shape, bf16),
            pltpu.VMEM(proj_hidden.shape, bf16),
            pltpu.VMEM(targets.shape, bf16),
            pltpu.VMEM((3, examples * rank, 2 * rank), bf16),
            pltpu.VMEM((tiles, TILE, tokens), f32),
            pltpu.VMEM((tiles, TILE, tokens), f32),
            pltpu.VMEM((n, TILE, tokens), f32),
            pltpu.VMEM((n, TILE, tokens), f32),
            pltpu.VMEM((TILE, tokens), f32),
            pltpu.VMEM((TILE, tokens), f32),
            pltpu.VMEM((tiles, TILE, tokens), f32),
            pltpu.VMEM((tiles, TILE, tokens), f32),
            pltpu.VMEM((SEQS * rank, 3 * tokens), bf16),
            pltpu.VMEM((2, examples * SEQS), f32),
            pltpu.VMEM((n, 2, examples * SEQS), f32),
            dma((3, CHUNKS)),
            dma((2, ROUTES)),
            dma((3,)),
            dma((ROUTES,)),
            dma((CHUNKS, ROUTES, stages)),
            dma((2,)),
            dma((2,)),
            dma((2,)),
            dma((2,)),
            dma(()),
            dma(()),
        ],
        compiler_params=pltpu.CompilerParams(
            collective_id=0, has_side_effects=True, vmem_limit_bytes=67000000
        ),
        name="sketch_scores",
    )(
        by_chunk(activations), by_chunk(cotangent), w_gate, w_up, w_down, proj_model, proj_hidden,
        seq_ids.reshape(1, tokens), targets, target_domain,
    )


def solution(mesh):
    in_specs = (
        P(("groups", "dp"), None),
        P(("groups", "dp"), None),
        P("dp", None),
        P("dp", None),
        P("dp", None),
        P("dp", None),
        P("dp", None),
        P("groups"),
        P(("groups", "dp"), None, None, None),
        P(("groups", "dp")),
    )
    out_specs = (P("groups", None, None, None), P("groups", None))
    return jax.shard_map(
        functools.partial(on_device, mesh.shape["dp"]),
        mesh=mesh, in_specs=in_specs, out_specs=out_specs, check_vma=False,
    )
```

```python
import functools

import jax
import jax.numpy as jnp
from jax import lax
from jax.experimental import pallas as pl
from jax.experimental.pallas import tpu as pltpu
from jax.sharding import PartitionSpec as P

DOMAINS = 32
SEQS = 16
MESH = pl.DeviceIdType.MESH
ROUTES = 2
CHUNKS = 16
GROUP = 2
EARLY = 0
LAG = 3
CORE_LAG = 2
TILE = 8


def routes_of(n):
    core = (2, 1)
    if n == 32:
        z, y, x = (4, 8), (2, 4), (2, 2)
        return ((z, y, x, core), (z, x, y, core), (y, z, x, core), (x, z, y, core))
    if n == 128:
        y, x = (8, 16), (8, 2)
        return ((y, x, core), (x, y, core)) * 2
    rest = (n // 2, 2)
    return ((rest, core),) * 4


def moved(index, size, stride, by):
    coord = lax.rem(lax.div(index, stride), size)
    return index + (lax.rem(coord + by, size) - coord) * stride


def kernel(
    n,
    act_ref, cot_ref, wg_ref, wu_ref, wd_ref, pm_ref, ph_ref, seq_ref, tgt_ref, dom_ref,
    vl_ref, vr_ref, mean_ref,
    wbuf, xg, xs, gacc, uacc, dacc, pm, ph, tgt, seqs, doms, tt, partl, partr, rsl, rsr, redl, redr, vl, vr, msg, msgbuf,
    w_sem, own_sem, in_sem, out_sem, ag_send, ag_recv, rs_send, rs_recv, bc_send, bc_recv, sc_send, sc_recv,
):
    me = lax.axis_index("dp")
    routes = routes_of(n)
    stages = len(routes[0])
    tokens, width = xs.shape[2], xs.shape[3]
    steps = xs.shape[1]
    part_width = width // (GROUP * ROUTES)
    rank = pm_ref.shape[0] // 3
    hidden_units = wg_ref.shape[0]
    own_rows = act_ref.shape[2]
    examples = tgt_ref.shape[0]
    tiles = partl.shape[0]

    def mult(r, stage):
        count = 1
        for size, _ in routes[r][:stage]:
            count = count * size
        return count

    def position(r, index, first=0):
        total = 0
        for i, (size, stride) in enumerate(routes[r]):
            if i >= first:
                if isinstance(index, int):
                    total += index // stride % size * mult(r, i)
                else:
                    total += lax.rem(lax.div(index, stride), size) * mult(r, i)
        return total

    def weight_copy(m, c):
        source = (wg_ref, wu_ref, wd_ref)[m]
        return pltpu.make_async_copy(
            source.at[:, pl.ds(c * width, width)], wbuf.at[m, c], w_sem.at[m, c]
        )

    own_copies = []
    for a, source in enumerate((act_ref, cot_ref)):
        for route in range(2 * ROUTES):
            r = route % ROUTES
            chunks = pl.ds(0, EARLY) if route >= ROUTES else pl.ds(EARLY, CHUNKS - EARLY)
            if chunks.size == 0:
                continue
            copy = pltpu.make_async_copy(
                source.at[chunks, r], xg.at[chunks, r, position(route, me), a], own_sem.at[a, route]
            )
            copy.start()
            own_copies.append(copy)

    barrier = pltpu.get_barrier_semaphore()
    partners = 0
    for size, stride in routes[0]:
        for d in range(1, size):
            pl.semaphore_signal(
                barrier, inc=1, device_id={"dp": moved(me, size, stride, d)}, device_id_type=MESH
            )
            partners += 1
    in_copies = [
        pltpu.make_async_copy(source, target, in_sem.at[i])
        for i, (source, target) in enumerate(
            ((pm_ref, pm), (ph_ref, ph), (tgt_ref, tgt), (seq_ref, seqs), (dom_ref, doms))
        )
    ]
    for m in range(3):
        weight_copy(m, 0).start()
    for copy in own_copies:
        copy.wait()
    pl.semaphore_wait(barrier, partners)

    def route_of(c, r):
        return r + ROUTES if isinstance(c, int) and c < EARLY else r

    def send_stage(c, r, stage):
        route = route_of(c, r)
        size, stride = routes[route][stage]
        blocks = xg.at[c, r, pl.ds(position(route, me, stage), mult(route, stage))]
        for d in range(1, size):
            pltpu.make_async_remote_copy(
                src_ref=blocks,
                dst_ref=blocks,
                send_sem=ag_send.at[r],
                recv_sem=ag_recv.at[c, r, stage],
                device_id={"dp": moved(me, size, stride, d)},
                device_id_type=MESH,
            ).start()

    def take_stage(c, r, stage):
        route = route_of(c, r)
        blocks = xg.at[c, r, pl.ds(0, mult(route, stage) * (routes[route][stage][0] - 1))]
        pltpu.make_async_copy(blocks, blocks, ag_recv.at[c, r, stage]).wait()

    def relay(c, stage):
        for r in range(ROUTES):
            take_stage(c, r, stage - 1)
            send_stage(c, r, stage)

    def first_sends(c, carry):
        for r in range(ROUTES):
            send_stage(c, r, 0)
        return carry

    def later_weights(c, carry):
        for m in range(3):
            weight_copy(m, c).start()
        return carry

    for c in range(EARLY):
        first_sends(c, 0)
    lax.fori_loop(EARLY, CHUNKS, first_sends, 0)
    lax.fori_loop(1, steps, later_weights, 0)
    for copy in in_copies:
        copy.start()
    gacc[...] = jnp.zeros_like(gacc)
    uacc[...] = jnp.zeros_like(uacc)
    dacc[...] = jnp.zeros_like(dacc)

    def lay_out(a, c):
        group = 16 // own_rows
        for part in range(GROUP * ROUTES):
            h, r = part // ROUTES, part % ROUTES
            for g in range(tokens // 16):
                pieces = [
                    xg[c * GROUP + h, r, position(route_of(c * GROUP + h, r), g * group + i), a].astype(jnp.float32)
                    for i in range(group)
                ]
                xs[a, c, g * 16 : (g + 1) * 16, part * part_width : (part + 1) * part_width] = (
                    jnp.concatenate(pieces, 0).astype(jnp.bfloat16)
                )

    contract = (((1,), (1,)), ((), ()))

    def add_product(acc, a, m, c):
        weight_copy(m, c).wait()
        acc[...] += lax.dot_general(
            wbuf[m, c], xs[a, c], contract, preferred_element_type=jnp.float32
        )

    def tick(i):
        for stage in range(1, stages):
            c = i - (stage - 1) * LAG
            if not isinstance(c, int):
                pl.when(c < CHUNKS)(functools.partial(relay, c, stage))
            elif 0 <= c < CHUNKS:
                relay(c, stage)

    ahead = GROUP - 1 + (stages - 2) * LAG + CORE_LAG
    for i in range(ahead):
        tick(i)

    def step(c, carry):
        tick(c * GROUP + ahead)
        for h in range(GROUP):
            for r in range(ROUTES):
                take_stage(c * GROUP + h, r, stages - 1)
        lay_out(0, c)
        add_product(gacc, 0, 0, c)
        tick(c * GROUP + ahead + 1)
        add_product(uacc, 0, 1, c)
        lay_out(1, c)
        add_product(dacc, 1, 2, c)
        return carry

    for c in range(EARLY // GROUP):
        step(c, 0)
    lax.fori_loop(EARLY // GROUP, steps, step, 0)

    for copy in in_copies:
        copy.wait()
    window = pm_ref.shape[1]
    model_cols = steps * width // n
    start = lax.div(me * model_cols, window) * window
    own_chunk = lax.div(start, width)
    own_cols = pl.ds(pl.multiple_of(lax.rem(start, width), window), window)

    def tiled(x):
        return x.reshape(x.shape[0] // TILE, TILE, tokens)

    split = 2 * rank // TILE
    partr[:split] = tiled(
        lax.dot_general(
            pm[: 2 * rank, :], xs[0, own_chunk, :, own_cols], contract, preferred_element_type=jnp.float32
        )
    )
    partr[split:] = tiled(
        lax.dot_general(
            pm[2 * rank :, :], xs[1, own_chunk, :, own_cols], contract, preferred_element_type=jnp.float32
        )
    )

    def owner_of(side, tile):
        owner = lax.div(tile * n, tiles)
        return n - 1 - owner if side else owner

    def side_of(side):
        index = n - 1 - me if side else me
        part, rsbuf, red, v = ((partl, rsl, redl, vl), (partr, rsr, redr, vr))[side]
        mine = lax.div(index * tiles + n - 1, n)
        reduces = lax.div(mine * n, tiles) == index
        return part, rsbuf, red, v, lax.rem(mine, tiles), reduces

    def scatter(side):
        part, rsbuf, _, _, mine, reduces = side_of(side)

        def send(tile):
            pltpu.make_async_remote_copy(
                src_ref=part.at[tile],
                dst_ref=rsbuf.at[me],
                send_sem=rs_send.at[side],
                recv_sem=rs_recv.at[side],
                device_id={"dp": owner_of(side, tile)},
                device_id_type=MESH,
            ).start()

        def one(d, carry):
            send(lax.rem(mine + d, tiles))
            return carry

        lax.fori_loop(1, tiles, one, 0, unroll=True)

        @pl.when(reduces)
        def _():
            pltpu.make_async_copy(part.at[mine], rsbuf.at[me], rs_recv.at[side]).start()

        @pl.when(jnp.logical_not(reduces))
        def _():
            send(mine)

    def share(side):
        part, rsbuf, red, v, mine, reduces = side_of(side)

        @pl.when(reduces)
        def _():
            pltpu.make_async_copy(rsbuf, rsbuf, rs_recv.at[side]).wait()
            red[...] = jnp.sum(rsbuf[...], 0)
            pltpu.make_async_copy(red, v.at[mine], bc_recv.at[side]).start()

            def one(d, carry):
                pltpu.make_async_remote_copy(
                    src_ref=red,
                    dst_ref=v.at[mine],
                    send_sem=bc_send.at[side],
                    recv_sem=bc_recv.at[side],
                    device_id={"dp": lax.rem(me + d, n)},
                    device_id_type=MESH,
                ).start()
                return carry

            lax.fori_loop(1, n, one, 0, unroll=n <= 32)

    def settle(side):
        part, rsbuf, red, v, _, reduces = side_of(side)

        @pl.when(reduces)
        def _():
            sent = part.at[pl.ds(0, tiles - 1)]
            pltpu.make_async_copy(sent, sent, rs_send.at[side]).wait()
            sent = rsbuf.at[pl.ds(0, n - 1)]
            pltpu.make_async_copy(sent, sent, bc_send.at[side]).wait()

        @pl.when(jnp.logical_not(reduces))
        def _():
            pltpu.make_async_copy(part, part, rs_send.at[side]).wait()

    scatter(1)
    in_down = out_gate = out_up = jnp.zeros((rank, tokens), jnp.float32)
    for off in range(0, hidden_units, 256):
        rows = slice(off, min(off + 256, hidden_units))
        gate, up, grad = gacc[rows], uacc[rows], dacc[rows]
        sig = jax.nn.sigmoid(gate)
        silu = gate * sig
        hidden = (silu * up).astype(jnp.bfloat16)
        grad_gate = (grad * up * sig * (1.0 + gate * (1.0 - sig))).astype(jnp.bfloat16)
        grad_up = (grad * silu).astype(jnp.bfloat16)
        in_down += jnp.dot(ph[:rank, rows], hidden, preferred_element_type=jnp.float32)
        out_gate += jnp.dot(ph[rank : 2 * rank, rows], grad_gate, preferred_element_type=jnp.float32)
        out_up += jnp.dot(ph[2 * rank :, rows], grad_up, preferred_element_type=jnp.float32)
    third = rank // TILE
    partl[:third] = tiled(out_gate)
    partl[third : 2 * third] = tiled(out_up)
    partl[2 * third :] = tiled(in_down)
    scatter(0)

    for e in range(examples):
        for k in range(3):
            piece = tgt[e, k].astype(jnp.float32)
            tt[k, e * rank : (e + 1) * rank, :] = jnp.concatenate([piece, piece], 1).astype(jnp.bfloat16)
    share(1)
    share(0)
    seq = seqs[...]
    lanes = lax.broadcasted_iota(jnp.int32, (1, examples * SEQS), 1)
    domains = jnp.zeros((1, examples * SEQS), jnp.int32)
    for e in range(examples):
        domains = jnp.where(lax.div(lanes, SEQS) == e, doms[e], domains)
    msg[1:2] = domains.astype(jnp.float32)
    same = lax.broadcasted_iota(jnp.int32, (examples * SEQS, tokens), 0)
    same = jnp.where(lax.rem(same, SEQS) == seq, 1.0, 0.0).astype(jnp.bfloat16)

    pltpu.make_async_copy(vr, vr, bc_recv.at[1]).wait()
    out_copies = [
        pltpu.make_async_copy(v, out, out_sem.at[side])
        for side, (v, out) in enumerate(((vl, vl_ref), (vr, vr_ref)))
    ]
    out_copies[1].start()
    products = []
    for k in range(3):
        right = vr[k * third : (k + 1) * third].reshape(rank, tokens)
        hi = right.astype(jnp.bfloat16)
        lo = (right - hi.astype(jnp.float32)).astype(jnp.bfloat16)
        products.append(
            jnp.dot(tt[k], jnp.concatenate([hi, lo], 0), preferred_element_type=jnp.float32)
        )
    pltpu.make_async_copy(vl, vl, bc_recv.at[0]).wait()
    out_copies[0].start()
    lefts = [vl[k * third : (k + 1) * third].reshape(rank, tokens) for k in range(3)]
    terms = jnp.zeros((examples, rank, tokens), jnp.float32)
    for k in range(3):
        terms += products[k].reshape(examples, rank, tokens) * lefts[k][None]
    term = jnp.sum(terms, 1)
    term_hi = term.astype(jnp.bfloat16).astype(jnp.float32)
    term_mid = (term - term_hi).astype(jnp.bfloat16).astype(jnp.float32)
    term_lo = term - term_hi - term_mid
    summed = lax.dot_general(
        jnp.concatenate([term_hi, term_mid, term_lo], 0).astype(jnp.bfloat16), same, contract,
        preferred_element_type=jnp.float32,
    )
    summed = summed[:examples] + summed[examples : 2 * examples] + summed[2 * examples :]
    row = lax.broadcasted_iota(jnp.int32, summed.shape, 0)
    lane = lax.broadcasted_iota(jnp.int32, summed.shape, 1)
    msg[0:1] = jnp.sum(jnp.where(lax.div(lane, SEQS) == row, summed, 0.0), 0, keepdims=True)
    pltpu.make_async_copy(msg, msgbuf.at[me], sc_recv).start()

    def spread(d, carry):
        pltpu.make_async_remote_copy(
            src_ref=msg,
            dst_ref=msgbuf.at[me],
            send_sem=sc_send,
            recv_sem=sc_recv,
            device_id={"dp": lax.rem(me + d, n)},
            device_id_type=MESH,
        ).start()
        return carry

    lax.fori_loop(1, n, spread, 0, unroll=n <= 32)

    for side in range(2):
        settle(side)

    def sent_chunk(c, carry):
        for r in range(ROUTES):
            sent = xg.at[c, r, pl.ds(0, n - 1)]
            pltpu.make_async_copy(sent, sent, ag_send.at[r]).wait()
        return carry

    lax.fori_loop(0, CHUNKS, sent_chunk, 0)
    sent = msgbuf.at[pl.ds(0, n - 1)]
    pltpu.make_async_copy(sent, sent, sc_send).wait()
    pltpu.make_async_copy(msgbuf, msgbuf, sc_recv).wait()
    domain = lax.broadcasted_iota(jnp.int32, (DOMAINS, examples * SEQS), 0).astype(jnp.float32)
    total = jnp.zeros(domain.shape, jnp.float32)
    counts = jnp.zeros(domain.shape, jnp.float32)
    for i in range(n):
        got = msgbuf[i]
        here = got[1:2] == domain
        total += jnp.where(here, got[0:1], 0.0)
        counts += jnp.where(here, 1.0, 0.0)
    shift = SEQS
    while shift < examples * SEQS:
        total += pltpu.roll(total, shift, 1)
        counts += pltpu.roll(counts, shift, 1)
        shift *= 2
    mean_ref[...] = total / counts
    for copy in out_copies:
        copy.wait()


def finish(vl_ref, vr_ref, mean_ref, seq_ref, sk_ref, score_ref, lm, held, sem):
    tokens = seq_ref.shape[1]
    rank = sk_ref.shape[3]
    third = rank // TILE
    contract = (((1,), (1,)), ((), ()))
    seq = seq_ref[...]
    squares = jnp.zeros((SEQS, TILE, rank), jnp.float32)
    copies = []
    for k in range(3):
        left = vl_ref[k * third : (k + 1) * third].reshape(rank, tokens)
        right = vr_ref[k * third : (k + 1) * third].reshape(rank, tokens)
        right_hi = right.astype(jnp.bfloat16)
        right_lo = (right - right_hi.astype(jnp.float32)).astype(jnp.bfloat16)
        left_hi = left.astype(jnp.bfloat16).astype(jnp.float32)
        left_lo = left - left_hi
        for s in range(SEQS):
            here = seq == s
            hi = jnp.where(here, left_hi, 0.0).astype(jnp.bfloat16)
            lo = jnp.where(here, left_lo, 0.0).astype(jnp.bfloat16)
            block = slice(s * rank, (s + 1) * rank)
            lm[block, :tokens] = hi
            lm[block, tokens : 2 * tokens] = lo
            lm[block, 2 * tokens :] = hi
        sketch = lax.dot_general(
            lm[...], jnp.concatenate([right_hi, right_hi, right_lo], 1), contract,
            preferred_element_type=jnp.float32,
        ).reshape(SEQS, rank, rank)
        held[k] = sketch
        copies.append(pltpu.make_async_copy(held.at[k], sk_ref.at[:, k], sem.at[k]))
        copies[k].start()
        for i in range(0, rank, TILE):
            piece = sketch[:, i : i + TILE]
            squares = squares + piece * piece
    inverse_norm = lax.rsqrt(jnp.sum(jnp.sum(squares, 1), 1, keepdims=True) + 1e-06)
    score_ref[...] = mean_ref[...].T[:SEQS] * inverse_norm
    for copy in copies:
        copy.wait()


def on_device(n, activations, cotangent, w_gate, w_up, w_down, proj_model, proj_hidden, seq_ids, targets, target_domain):
    own_rows, model = activations.shape
    tokens = n * own_rows
    hidden_units = w_gate.shape[0]
    model_cols, features = proj_model.shape
    rank = features // 3
    steps = CHUNKS // GROUP
    width = model // steps
    part_width = width // (GROUP * ROUTES)
    stages = len(routes_of(n)[0])
    examples = targets.shape[0]
    tiles = features // TILE

    def by_chunk(x):
        return x.reshape(own_rows, CHUNKS, ROUTES, part_width).transpose(1, 2, 0, 3)

    proj_model, proj_hidden = proj_model.T, proj_hidden.T
    if model_cols < 128:
        me = lax.axis_index("dp")
        padded = jnp.zeros((features, 128), proj_model.dtype)
        proj_model = lax.dynamic_update_slice(padded, proj_model, (0, (me * model_cols) % 128))
    vmem = pl.BlockSpec(memory_space=pltpu.VMEM)
    hbm = pl.BlockSpec(memory_space=pl.ANY)
    f32, bf16 = jnp.float32, jnp.bfloat16
    dma = pltpu.SemaphoreType.DMA
    sequences = seq_ids.reshape(1, tokens)
    lefts, rights, means = pl.pallas_call(
        functools.partial(kernel, n),
        out_shape=(
            jax.ShapeDtypeStruct((tiles, TILE, tokens), f32),
            jax.ShapeDtypeStruct((tiles, TILE, tokens), f32),
            jax.ShapeDtypeStruct((DOMAINS, examples * SEQS), f32),
        ),
        in_specs=[hbm] * 10,
        out_specs=(hbm, hbm, vmem),
        scratch_shapes=[
            pltpu.VMEM((3, steps, hidden_units, width), bf16),
            pltpu.VMEM((CHUNKS, ROUTES, n, 2, own_rows, part_width), bf16),
            pltpu.VMEM((2, steps, tokens, width), bf16),
            pltpu.VMEM((hidden_units, tokens), f32),
            pltpu.VMEM((hidden_units, tokens), f32),
            pltpu.VMEM((hidden_units, tokens), f32),
            pltpu.VMEM(proj_model.shape, bf16),
            pltpu.VMEM(proj_hidden.shape, bf16),
            pltpu.VMEM(targets.shape, bf16),
            pltpu.VMEM((1, tokens), jnp.int32),
            pltpu.SMEM((examples,), jnp.int32),
            pltpu.VMEM((3, examples * rank, 2 * rank), bf16),
            pltpu.VMEM((tiles, TILE, tokens), f32),
            pltpu.VMEM((tiles, TILE, tokens), f32),
            pltpu.VMEM((n, TILE, tokens), f32),
            pltpu.VMEM((n, TILE, tokens), f32),
            pltpu.VMEM((TILE, tokens), f32),
            pltpu.VMEM((TILE, tokens), f32),
            pltpu.VMEM((tiles, TILE, tokens), f32),
            pltpu.VMEM((tiles, TILE, tokens), f32),
            pltpu.VMEM((2, examples * SEQS), f32),
            pltpu.VMEM((n, 2, examples * SEQS), f32),
            dma((3, steps)),
            dma((2, 2 * ROUTES)),
            dma((5,)),
            dma((2,)),
            dma((ROUTES,)),
            dma((CHUNKS, ROUTES, stages)),
            dma((2,)),
            dma((2,)),
            dma((2,)),
            dma((2,)),
            dma(()),
            dma(()),
        ],
        compiler_params=pltpu.CompilerParams(
            collective_id=0, has_side_effects=True, vmem_limit_bytes=67000000
        ),
        name="sketch_scores",
    )(
        by_chunk(activations), by_chunk(cotangent), w_gate, w_up, w_down, proj_model, proj_hidden,
        sequences, targets, target_domain,
    )
    return pl.pallas_call(
        finish,
        out_shape=(
            jax.ShapeDtypeStruct((SEQS, 3, rank, rank), f32),
            jax.ShapeDtypeStruct((SEQS, DOMAINS), f32),
        ),
        in_specs=[vmem] * 4,
        out_specs=(hbm, vmem),
        scratch_shapes=[
            pltpu.VMEM((SEQS * rank, 3 * tokens), bf16),
            pltpu.VMEM((3, SEQS, rank, rank), f32),
            dma((3,)),
        ],
        name="finish",
    )(lefts, rights, means, sequences)


def solution(mesh):
    in_specs = (
        P(("groups", "dp"), None),
        P(("groups", "dp"), None),
        P("dp", None),
        P("dp", None),
        P("dp", None),
        P("dp", None),
        P("dp", None),
        P("groups"),
        P(("groups", "dp"), None, None, None),
        P(("groups", "dp")),
    )
    out_specs = (P("groups", None, None, None), P("groups", None))
    return jax.shard_map(
        functools.partial(on_device, mesh.shape["dp"]),
        mesh=mesh, in_specs=in_specs, out_specs=out_specs, check_vma=False,
    )
```
